128 devices in a mesh: expert: 64 (over x, z, y), replica: 2 (over core).
Axes of the slice: x: 4, y: 4, z: 4, core: 2. Of those that a mesh axis runs over, the one named last changes fastest.
Arguments:
- tokens: bfloat16 [65536, 1024], P(('expert', 'replica')), may hold values from -6 to 6
- expert_id: int32 [65536, 1], P(('expert', 'replica')), may hold values from 0 to 63; in each aligned block of 512 rows (0 to 511, 512 to 1023, ...) at most 16 rows name the same one
- router_prob: float32 [65536], P(('expert', 'replica')), may hold values from 0.1 to 1
- keep_mask: int32 [64, 128, 2048], P('expert'), may hold values 0 or 1
- w_in: bfloat16 [64, 1024, 2048], P('expert'), may hold values from -0.1875 to 0.1875
- w_out: bfloat16 [64, 2048, 1024], P('expert'), may hold values from -0.125 to 0.125
- cotangent: bfloat16 [65536, 1024], P(('expert', 'replica')), may hold values from -0.59765625 to 0.59765625
Outputs:
- mixed: bfloat16 [65536, 1024], P(('expert', 'replica'))
- grad_in: float32 [64, 1024, 2048], P('expert', 'replica')
- grad_out: float32 [64, 2048, 1024], P('expert', 'replica')
The draws below stay inside these ranges and needn't reach their ends.
Inputs may be any that keep to these rules, and one draw needn't show every extreme that they name: `expert_id`: among the 512 tokens of one device no expert is chosen more than 16 times; on some devices one expert is chosen exactly 16 times.
All inputs are finite; a program needn't handle non-finite values. No bound on the sum of `keep_mask` on one device may be relied on, other than what follows from the above.
Results may differ from the reference program's by a relative error of at most 0.0057.
Values may be sent and summed in bfloat16 or wider, within the bound.
No kernel may reach another device: no remote copies, remote signals or barrier semaphores. Data moves between devices by JAX's collectives and lax.ppermute only.
A program may use at most 128 MiB of HBM per device.

```python
import math
import jax
import jax.numpy as jnp
import numpy as np
from jax import lax

D = 1024
FF = 2048
TOK_DEV = 512
EXPERTS = 64
SOURCES = 128
TOKENS = 65536
CAP = 16


def set_ends(result, key, smallest, largest):
    longest = result.shape.index(max(result.shape))
    spots = []
    for shift in (0, 1):
        where = [jax.random.randint(jax.random.fold_in(key, axis), (), 0, length) for axis, length in enumerate(result.shape)]
        where[longest] = (where[longest] + shift) % result.shape[longest]
        spots.append(tuple(where))
    return result.at[spots[0]].set(smallest).at[spots[1]].set(largest)


def level_of(own_key, dims, shards, low, high):
    def one(axis_at, parts):
        steps = jax.random.uniform(jax.random.fold_in(jax.random.fold_in(own_key, 6), axis_at), (parts,), jnp.float32, low / len(shards), high / len(shards))
        return jnp.repeat(jnp.exp(steps), dims[axis_at] // parts).reshape((-1,) + (1,) * (len(dims) - axis_at - 1))

    gain = one(*shards[0])
    for cut in shards[1:]:
        gain = gain * one(*cut)
    return gain


def deal_out(own_key, own, number, rows, count, top, limit, skew):
    ranking = jax.random.permutation(own_key, count)
    packed, common = portions_of(count, rows * top, limit, skew, True), portions_of(count, rows * top, limit, skew, False)
    places = jnp.arange(count)

    def named(sizes, rotation):
        used = int((sizes > 0).sum())
        fixed = max(1, used // 4)
        shifted = fixed + (places - fixed + rotation * (used - fixed)) % max(1, count - fixed)
        return jnp.zeros((count,), jnp.int32).at[ranking[jnp.where(places < fixed, places, shifted)]].set(jnp.asarray(sizes, jnp.int32))

    sizes = jnp.where(number % 4 == 0, named(packed, number // 4), named(common, number - number // 4 - 1))
    mixed = jax.random.permutation(jax.random.fold_in(own, 3), count)
    giver, taker = mixed[0:count // 2 * 2:2], mixed[1:count // 2 * 2:2]
    room = jnp.minimum(sizes[giver] - 1, limit - sizes[taker]) // 2
    room = jnp.where((giver == ranking[0]) | (taker == ranking[0]) | (sizes[taker] == 0), 0, jnp.maximum(room, 0))
    shifted = jax.random.randint(jax.random.fold_in(own, 4), (count // 2,), 0, 1 << 20) % (room + 1)
    sizes = sizes.at[giver].add(-shifted).at[taker].add(shifted)
    items = jnp.searchsorted(jnp.cumsum(sizes), jnp.arange(rows * top), side="right").astype(jnp.int32)
    listing = items.reshape(top, rows).T
    listing = listing[jax.random.permutation(jax.random.fold_in(own, 1), rows)]
    rotation = jax.random.randint(jax.random.fold_in(own, 2), (rows, 1), 0, top)
    return jnp.take_along_axis(listing, (jnp.arange(top)[None, :] + rotation) % top, axis=1)


def portions_of(number_of, total, reach, skew, full):
    weights = [(1 << 20) // math.isqrt(grade ** skew) + 1 for grade in range(1, number_of + 1)]
    largest = reach if full else min(reach, max(-(-total // number_of), total * weights[0] // sum(weights)))
    least = 1 if total - largest >= number_of - 1 else 0
    holding, surplus = [largest] + [least] * (number_of - 1), total - largest - least * (number_of - 1)
    while surplus > 0:
        candidates = [i for i in range(1, number_of) if holding[i] < largest] or [i for i in range(1, number_of) if holding[i] < reach]
        whole, remaining = sum([weights[i] for i in candidates]), surplus
        for i in candidates:
            extra = min(reach - holding[i], max(1, remaining * weights[i] // whole), surplus)
            holding[i] = holding[i] + extra
            surplus = surplus - extra
    return np.array(holding)


def centred(own_key, dims, deviation, most, pieces=(), kind=jnp.bfloat16):
    loudness = level_of(own_key, dims, pieces, -0.22, 0.18) if pieces else 1.0
    drawn = jax.random.normal(own_key, dims, jnp.float32) * deviation * loudness
    return jnp.minimum(jnp.maximum(drawn, -most), most).astype(kind)


def setup_inputs(seed: int = 0) -> dict:
    splits = jax.random.split(jax.random.key(seed), 8)
    tokens = centred(splits[0], (TOKENS, D), 1.0, 6.0, ((0, 128),))
    expert_id_keys = jax.random.split(jax.random.fold_in(splits[1], 1), TOKENS // TOK_DEV)
    expert_id_turns = jax.random.permutation(jax.random.fold_in(splits[1], 3), TOKENS // TOK_DEV)
    expert_id = jax.vmap(lambda own, number: deal_out(jax.random.fold_in(splits[1], 2), own, number, TOK_DEV, EXPERTS, 1, CAP, 2))(expert_id_keys, expert_id_turns).reshape((TOKENS, 1))
    router_prob = jnp.clip(0.1 + 0.9 * jax.random.uniform(splits[2], (TOKENS,), jnp.float32) ** level_of(splits[2], (TOKENS,), ((0, 128),), -0.2, 0.2), 0.1, 1.0)
    keep_mask = set_ends((jax.random.randint(splits[3], (EXPERTS, SOURCES, FF), 0, 4) < 3).astype(jnp.int32), jax.random.fold_in(splits[3], 1), 0, 1)
    w_in = centred(splits[4], (EXPERTS, D, FF), D ** -0.5, 0.1875, ((0, 64),))
    w_out = centred(splits[5], (EXPERTS, FF, D), FF ** -0.5, 0.125, ((0, 64),))
    cotangent = centred(splits[6], (TOKENS, D), 0.1, 0.59765625, ((0, 128),))
    return dict(tokens=tokens, expert_id=expert_id, router_prob=router_prob, keep_mask=keep_mask, w_in=w_in, w_out=w_out, cotangent=cotangent)


KEEP_SCALE = 4.0 / 3.0


def gelu_parts(pre):
    inner = 0.7978845608 * (pre + 0.044715 * pre * pre * pre)
    tanh_v = jnp.tanh(inner)
    value = 0.5 * pre * (1.0 + tanh_v)
    slope = 0.5 * (1.0 + tanh_v) + 0.5 * pre * (1.0 - tanh_v * tanh_v) * 0.7978845608 * (1.0 + 3.0 * 0.044715 * pre * pre)
    return value, slope


def reference(tokens, expert_id, router_prob, keep_mask, w_in, w_out, cotangent):
    ids = expert_id[:, 0].astype(jnp.int32)
    per = ids.reshape(SOURCES, TOK_DEV)
    onehot = (per[:, :, None] == jnp.arange(EXPERTS, dtype=jnp.int32)[None, None, :]).astype(jnp.int32)
    rank = (jnp.sum(jnp.cumsum(onehot, axis=1) * onehot, axis=2) - 1).reshape(TOKENS).astype(jnp.int32)
    source = (jnp.arange(TOKENS, dtype=jnp.int32) // TOK_DEV).astype(jnp.int32)
    place = (ids * (SOURCES * CAP) + source * CAP + rank).astype(jnp.int32)
    table = jnp.full((EXPERTS * SOURCES * CAP,), TOKENS, jnp.int32).at[place].set(jnp.arange(TOKENS, dtype=jnp.int32))
    table = table.reshape(EXPERTS, SOURCES * CAP)
    gated = (router_prob[:, None] * cotangent.astype(jnp.float32)).astype(jnp.bfloat16)
    x_pad = jnp.concatenate([tokens, jnp.zeros((1, D), tokens.dtype)], axis=0)
    g_pad = jnp.concatenate([gated, jnp.zeros((1, D), gated.dtype)], axis=0)

    def one_expert(args):
        index_row, weight_in, weight_out, keep_rows = args
        rows_x = x_pad[index_row]
        rows_g = g_pad[index_row]
        keep_scale = jnp.repeat(keep_rows.astype(jnp.float32) * KEEP_SCALE, CAP, axis=0)
        pre = jnp.dot(rows_x, weight_in, preferred_element_type=jnp.float32)
        value, slope = gelu_parts(pre)
        hidden = (value * keep_scale).astype(jnp.bfloat16)
        out = jnp.dot(hidden, weight_out, preferred_element_type=jnp.float32).astype(jnp.bfloat16)
        g_out = jnp.dot(hidden.T, rows_g, preferred_element_type=jnp.float32)
        dhidden = jnp.dot(rows_g, weight_out.T, preferred_element_type=jnp.float32)
        dpre = (dhidden * keep_scale * slope).astype(jnp.bfloat16)
        g_in = jnp.dot(rows_x.T, dpre, preferred_element_type=jnp.float32)
        return out, g_in, g_out

    outs, grad_in, grad_out = lax.map(one_expert, (table, w_in, w_out, keep_mask))
    flat = outs.reshape(EXPERTS * SOURCES * CAP, D)
    expert_out = flat[place]
    mixed = (router_prob[:, None] * expert_out.astype(jnp.float32)).astype(jnp.bfloat16)
    return mixed, grad_in, grad_out
```

```python
import jax
import jax.numpy as jnp
from jax import lax
from jax.sharding import PartitionSpec as P

KEEP_SCALE = 4.0 / 3.0
SWAP = [(0, 1), (1, 0)]


def gelu_parts(pre):
    inner = 0.7978845608 * (pre + 0.044715 * pre * pre * pre)
    tanh_v = jnp.tanh(inner)
    value = 0.5 * pre * (1.0 + tanh_v)
    slope = 0.5 * (1.0 + tanh_v) + 0.5 * pre * (1.0 - tanh_v * tanh_v) * 0.7978845608 * (
        1.0 + 3.0 * 0.044715 * pre * pre
    )
    return (value, slope)


def exchange(array):
    return lax.all_to_all(array, "expert", split_axis=0, concat_axis=0, tiled=True)


def summed_over_copies(rows, columns):
    half = rows.shape[1] // 2
    here = lax.axis_index("replica")

    def product(which):
        part = lax.dynamic_slice_in_dim(rows, which * half, half, axis=1)
        return lax.dot_general(
            part, columns, (((0,), (0,)), ((), ())), preferred_element_type=jnp.float32
        )

    other = lax.ppermute(product(1 - here).astype(jnp.bfloat16), "replica", SWAP)
    return product(here) + other.astype(jnp.float32)


def shards(tokens, expert_id, router_prob, keep_mask, w_in, w_out, cotangent):
    tok_rows, width = tokens.shape
    n_expert = lax.axis_size("expert")
    n_replica = lax.axis_size("replica")
    capacity = 2 * tok_rows // n_expert
    slots = n_expert * capacity
    weight_in = w_in[0]
    weight_out = w_out[0]
    ids = expert_id[:, 0]
    order = jnp.arange(tok_rows, dtype=jnp.int32)
    earlier = (ids[:, None] == ids[None, :]) & (order[None, :] < order[:, None])
    ranks = jnp.sum(earlier.astype(jnp.int32), axis=1)
    target = ids * capacity + ranks
    select = (target[:, None] == jnp.arange(slots, dtype=jnp.int32)[None, :]).astype(jnp.bfloat16)

    def fill_slots(values):
        filled = lax.dot_general(
            select, values, (((0,), (0,)), ((), ())), preferred_element_type=jnp.float32
        )
        return filled.astype(jnp.bfloat16).reshape(n_expert, capacity, width)

    received = exchange(fill_slots(tokens)).reshape(slots, width)
    gated = (router_prob[:, None] * cotangent.astype(jnp.float32)).astype(jnp.bfloat16)
    grad_rows = exchange(fill_slots(gated)).reshape(slots, width)
    keep_rows = lax.dynamic_index_in_dim(
        keep_mask[0].reshape(n_expert, n_replica, -1),
        lax.axis_index("replica"),
        axis=1,
        keepdims=False,
    )
    keep_scale = keep_rows.astype(jnp.float32) * KEEP_SCALE
    keep_scale = jnp.broadcast_to(keep_scale[:, None, :], (n_expert, capacity, keep_scale.shape[1]))
    keep_scale = keep_scale.reshape(slots, -1)
    pre = jnp.dot(received, weight_in, preferred_element_type=jnp.float32)
    value, slope = gelu_parts(pre)
    hidden = (value * keep_scale).astype(jnp.bfloat16)
    slope = slope * keep_scale
    out = jnp.dot(hidden, weight_out, preferred_element_type=jnp.float32).astype(jnp.bfloat16)
    back = exchange(out.reshape(n_expert, capacity, width)).reshape(slots, width)
    grad_out = summed_over_copies(hidden, grad_rows)
    dhidden = lax.dot_general(
        grad_rows, weight_out, (((1,), (1,)), ((), ())), preferred_element_type=jnp.float32
    )
    dpre = (dhidden * slope).astype(jnp.bfloat16)
    grad_in = summed_over_copies(received, dpre)
    expert_out = jnp.dot(select, back, preferred_element_type=jnp.float32)
    mixed = (router_prob[:, None] * expert_out).astype(jnp.bfloat16)
    return (mixed, grad_in[None], grad_out[None])


def solution(mesh):
    in_specs = (
        P(("expert", "replica"), None),
        P(("expert", "replica"), None),
        P(("expert", "replica")),
        P("expert", None, None),
        P("expert", None, None),
        P("expert", None, None),
        P(("expert", "replica"), None),
    )
    out_specs = (
        P(("expert", "replica"), None),
        P("expert", "replica", None),
        P("expert", "replica", None),
    )
    return jax.shard_map(shards, mesh=mesh, in_specs=in_specs, out_specs=out_specs, check_vma=False)
```

```python
import jax
import jax.numpy as jnp
from jax import lax
from jax.sharding import PartitionSpec as P

KEEP_SCALE = 4.0 / 3.0
SWAP = [(0, 1), (1, 0)]


def gelu_parts(pre):
    inner = 0.7978845608 * (pre + 0.044715 * pre * pre * pre)
    tanh_v = jnp.tanh(inner)
    value = 0.5 * pre * (1.0 + tanh_v)
    slope = 0.5 * (1.0 + tanh_v) + 0.5 * pre * (1.0 - tanh_v * tanh_v) * 0.7978845608 * (
        1.0 + 3.0 * 0.044715 * pre * pre
    )
    return (value, slope)


def exchange(array):
    return lax.all_to_all(array, "expert", split_axis=0, concat_axis=0, tiled=True)


def summed_over_copies(rows, columns):
    half = rows.shape[1] // 2
    here = lax.axis_index("replica")

    def product(which):
        part = lax.dynamic_slice_in_dim(rows, which * half, half, axis=1)
        return lax.dot_general(
            part, columns, (((0,), (0,)), ((), ())), preferred_element_type=jnp.float32
        )

    share = product(1 - here).astype(jnp.bfloat16)
    pieces = [lax.ppermute(piece, "replica", SWAP) for piece in jnp.split(share, 2, axis=0)]
    return product(here) + jnp.concatenate(pieces, axis=0).astype(jnp.float32)


def shards(tokens, expert_id, router_prob, keep_mask, w_in, w_out, cotangent):
    tok_rows, width = tokens.shape
    n_expert = lax.axis_size("expert")
    n_replica = lax.axis_size("replica")
    capacity = 2 * tok_rows // n_expert
    slots = n_expert * capacity
    weight_in = w_in[0]
    weight_out = w_out[0]
    ids = expert_id[:, 0]
    order = jnp.arange(tok_rows, dtype=jnp.int32)
    earlier = (ids[:, None] == ids[None, :]) & (order[None, :] < order[:, None])
    ranks = jnp.sum(earlier.astype(jnp.int32), axis=1)
    target = ids * capacity + ranks
    select = (target[:, None] == jnp.arange(slots, dtype=jnp.int32)[None, :]).astype(jnp.bfloat16)

    def fill_slots(values):
        filled = lax.dot_general(
            select, values, (((0,), (0,)), ((), ())), preferred_element_type=jnp.float32
        )
        return filled.astype(jnp.bfloat16).reshape(n_expert, capacity, width)

    gated = (router_prob[:, None] * cotangent.astype(jnp.float32)).astype(jnp.bfloat16)
    keep_rows = lax.dynamic_index_in_dim(
        keep_mask[0].reshape(n_expert, n_replica, -1),
        lax.axis_index("replica"),
        axis=1,
        keepdims=False,
    )
    keep_scale = keep_rows.astype(jnp.float32) * KEEP_SCALE
    sent = fill_slots(tokens)
    sent_grad = fill_slots(gated)
    received = exchange(sent).reshape(slots, width)
    sent_grad, keep_scale = lax.optimization_barrier((sent_grad, keep_scale))
    grad_rows = exchange(sent_grad).reshape(slots, width)
    keep_scale = jnp.broadcast_to(keep_scale[:, None, :], (n_expert, capacity, keep_scale.shape[1]))
    keep_scale = keep_scale.reshape(slots, -1)
    pre = jnp.dot(received, weight_in, preferred_element_type=jnp.float32)
    value, slope = gelu_parts(pre)
    hidden = (value * keep_scale).astype(jnp.bfloat16)
    slope = (slope * keep_scale).astype(jnp.bfloat16)
    out = jnp.dot(hidden, weight_out, preferred_element_type=jnp.float32).astype(jnp.bfloat16)
    out, grad_rows = lax.optimization_barrier((out, grad_rows))
    back = exchange(out.reshape(n_expert, capacity, width)).reshape(slots, width)
    grad_out = summed_over_copies(hidden, grad_rows)
    dhidden = lax.dot_general(
        grad_rows, weight_out, (((1,), (1,)), ((), ())), preferred_element_type=jnp.float32
    )
    dpre = (dhidden * slope.astype(jnp.float32)).astype(jnp.bfloat16)
    grad_in = summed_over_copies(received, dpre)
    back, grad_in, grad_out = lax.optimization_barrier((back, grad_in, grad_out))
    expert_out = jnp.dot(select, back, preferred_element_type=jnp.float32)
    mixed = (router_prob[:, None] * expert_out).astype(jnp.bfloat16)
    return (mixed, grad_in[None], grad_out[None])


def solution(mesh):
    in_specs = (
        P(("expert", "replica"), None),
        P(("expert", "replica"), None),
        P(("expert", "replica")),
        P("expert", None, None),
        P("expert", None, None),
        P("expert", None, None),
        P(("expert", "replica"), None),
    )
    out_specs = (
        P(("expert", "replica"), None),
        P("expert", "replica", None),
        P("expert", "replica", None),
    )
    return jax.shard_map(shards, mesh=mesh, in_specs=in_specs, out_specs=out_specs, check_vma=False)
```

```python
import functools

import jax
import jax.numpy as jnp
from jax import lax
from jax.experimental import pallas as pl
from jax.experimental.pallas import tpu as pltpu
from jax.sharding import PartitionSpec as P

KEEP_SCALE = 4.0 / 3.0
SWAP = [(0, 1), (1, 0)]
TN = (((0,), (0,)), ((), ()))
NT = (((1,), (1,)), ((), ()))
CHUNKS = 4
PARAMS = pltpu.CompilerParams(vmem_limit_bytes=16 * 2**20)
VMEM = pl.BlockSpec(memory_space=pltpu.VMEM)
SMEM = pl.BlockSpec(memory_space=pltpu.SMEM)


def resident(array):
    return pltpu.with_memory_space_constraint(array, pltpu.VMEM)


def cut(ref, dim, index, count):
    size = ref.shape[dim] // count
    part = pl.ds(index * size, size)
    return ref.at[part, :] if dim == 0 else ref.at[:, part]


def half_of(ref, which):
    half = ref.shape[1] // 2
    return ref.at[:, pl.ds(pl.multiple_of(which * half, half), half)]


def part_of_product(dim, c, rows, columns):
    left, right = (cut(rows, 1, c, CHUNKS), columns) if dim == 0 else (rows, cut(columns, 1, c, CHUNKS))
    return lax.dot_general(left[...], right[...], TN, preferred_element_type=jnp.float32)


def far_kernel(dim, which_ref, rows, columns, *outs):
    half = rows.shape[1] // 2
    for c in range(CHUNKS):
        total = part_of_product(dim, c, half_of(rows, which_ref[0]), columns)
        cut(outs[c // 2], dim, c % 2, 2)[...] = total.astype(jnp.bfloat16)


def near_kernel(dim, which_ref, rows, columns, first, second, out_hbm, out, sem):
    departures = []
    for c in range(CHUNKS):
        far = cut((first, second)[c // 2], dim, c % 2, 2)
        total = part_of_product(dim, c, half_of(rows, which_ref[0]), columns)
        cut(out, dim, c, CHUNKS)[...] = total + far[...].astype(jnp.float32)
        departure = pltpu.make_async_copy(
            cut(out, dim, c, CHUNKS), cut(out_hbm, dim, c, CHUNKS), sem.at[c]
        )
        departure.start()
        departures.append(departure)
    for departure in departures:
        departure.wait()


def half_product(which, rows, columns, dim, far=None):
    half, wide = rows.shape[1] // 2, columns.shape[1]
    if far is None:
        piece = (half // 2, wide) if dim == 0 else (half, wide // 2)
        return pl.pallas_call(
            functools.partial(far_kernel, dim),
            out_shape=[pltpu.VMEM(piece, jnp.bfloat16)] * 2,
            in_specs=[SMEM, VMEM, VMEM],
            out_specs=[VMEM] * 2,
            compiler_params=PARAMS,
            name="far_product",
        )(which, resident(rows), resident(columns))
    return pl.pallas_call(
        functools.partial(near_kernel, dim),
        out_shape=jax.ShapeDtypeStruct((half, wide), jnp.float32),
        in_specs=[SMEM] + [VMEM] * 4,
        out_specs=pl.BlockSpec(memory_space=pl.ANY),
        scratch_shapes=[
            pltpu.VMEM((half, wide), jnp.float32),
            pltpu.SemaphoreType.DMA((CHUNKS,)),
        ],
        compiler_params=PARAMS,
        name="near_product",
    )(which, resident(rows), resident(columns), resident(far[0]), resident(far[1]))


def backward_kernel(which_ref, grads, weight, slope, rows, dpre, *far):
    depth = grads.shape[0]
    for c in range(CHUNKS):
        for r in range(4):
            dhidden = lax.dot_general(
                cut(grads, 0, r, 4)[...], cut(weight, 0, c, CHUNKS)[...], NT, preferred_element_type=jnp.float32
            )
            factor = cut(cut(slope, 1, c, CHUNKS), 0, r, 4)[...].astype(jnp.float32)
            cut(cut(dpre, 1, c, CHUNKS), 0, r, 4)[...] = (dhidden * factor).astype(jnp.bfloat16)
        share = part_of_product(1, c, half_of(rows, which_ref[0]), dpre)
        cut(far[c // 2], 1, c % 2, 2)[...] = share.astype(jnp.bfloat16)


def backward(which, grads, weight, slope, rows):
    depth, width = grads.shape
    hidden, half = slope.shape[1], width // 2
    piece = pltpu.VMEM((half, hidden // 2), jnp.bfloat16)
    return pl.pallas_call(
        backward_kernel,
        out_shape=[pltpu.VMEM((depth, hidden), jnp.bfloat16), piece, piece],
        in_specs=[SMEM] + [VMEM] * 4,
        out_specs=[VMEM] * 3,
        compiler_params=PARAMS,
        name="backward",
    )(which, *map(resident, (grads, weight, slope, rows)))


def gelu_parts(pre):
    inner = 0.7978845608 * (pre + 0.044715 * pre * pre * pre)
    tanh_v = jnp.tanh(inner)
    value = 0.5 * pre * (1.0 + tanh_v)
    slope = 0.5 * (1.0 + tanh_v) + 0.5 * pre * (1.0 - tanh_v * tanh_v) * 0.7978845608 * (
        1.0 + 3.0 * 0.044715 * pre * pre
    )
    return (value, slope)


def exchange(array):
    return lax.all_to_all(array, "expert", split_axis=0, concat_axis=0, tiled=True)


def swapped(pieces):
    return [lax.ppermute(piece, "replica", SWAP) for piece in pieces]


def shards(tokens, expert_id, router_prob, keep_mask, w_in, w_out, cotangent):
    tok_rows, width = tokens.shape
    n_expert = lax.axis_size("expert")
    n_replica = lax.axis_size("replica")
    capacity = 2 * tok_rows // n_expert
    slots = n_expert * capacity
    weight_in = w_in[0]
    weight_out = w_out[0]
    ids = expert_id[:, 0]
    order = jnp.arange(tok_rows, dtype=jnp.int32)
    earlier = (ids[:, None] == ids[None, :]) & (order[None, :] < order[:, None])
    ranks = jnp.sum(earlier.astype(jnp.int32), axis=1)
    target = ids * capacity + ranks
    select = (target[:, None] == jnp.arange(slots, dtype=jnp.int32)[None, :]).astype(jnp.bfloat16)

    def fill_slots(values):
        filled = lax.dot_general(
            select, values, (((0,), (0,)), ((), ())), preferred_element_type=jnp.float32
        )
        return filled.astype(jnp.bfloat16).reshape(n_expert, capacity, width)

    gated = (router_prob[:, None] * cotangent.astype(jnp.float32)).astype(jnp.bfloat16)
    keep_rows = lax.dynamic_index_in_dim(
        keep_mask[0].reshape(n_expert, n_replica, -1),
        lax.axis_index("replica"),
        axis=1,
        keepdims=False,
    )
    keep_scale = keep_rows.astype(jnp.float32) * KEEP_SCALE
    sent = fill_slots(tokens)
    sent_grad = fill_slots(gated)
    received = exchange(sent).reshape(slots, width)
    sent_grad, keep_scale = lax.optimization_barrier((sent_grad, keep_scale))
    grad_rows = exchange(sent_grad).reshape(slots, width)
    keep_scale = jnp.broadcast_to(keep_scale[:, None, :], (n_expert, capacity, keep_scale.shape[1]))
    keep_scale = keep_scale.reshape(slots, -1)
    pre = jnp.dot(received, weight_in, preferred_element_type=jnp.float32)
    value, slope = gelu_parts(pre)
    hidden = (value * keep_scale).astype(jnp.bfloat16)
    slope = (slope * keep_scale).astype(jnp.bfloat16)
    out = jnp.dot(hidden, weight_out, preferred_element_type=jnp.float32).astype(jnp.bfloat16)
    out, grad_rows = lax.optimization_barrier((out, grad_rows))
    back = exchange(out.reshape(n_expert, capacity, width)).reshape(slots, width)
    here = lax.axis_index("replica").reshape(1)
    other = 1 - here
    dpre, *far_in = backward(other, grad_rows, weight_out, slope, received)
    far_in = swapped(far_in)
    far_out = swapped(half_product(other, hidden, grad_rows, 0))
    grad_in = half_product(here, received, dpre, 1, far_in)
    grad_out = half_product(here, hidden, grad_rows, 0, far_out)
    back, grad_in, grad_out = lax.optimization_barrier((back, grad_in, grad_out))
    expert_out = jnp.dot(select, back, preferred_element_type=jnp.float32)
    mixed = (router_prob[:, None] * expert_out).astype(jnp.bfloat16)
    return (mixed, grad_in[None], grad_out[None])


def solution(mesh):
    in_specs = (
        P(("expert", "replica"), None),
        P(("expert", "replica"), None),
        P(("expert", "replica")),
        P("expert", None, None),
        P("expert", None, None),
        P("expert", None, None),
        P(("expert", "replica"), None),
    )
    out_specs = (
        P(("expert", "replica"), None),
        P("expert", "replica", None),
        P("expert", "replica", None),
    )
    return jax.shard_map(shards, mesh=mesh, in_specs=in_specs, out_specs=out_specs, check_vma=False)
```

```python
import functools

import jax
import jax.numpy as jnp
from jax import lax
from jax.experimental import pallas as pl
from jax.experimental.pallas import tpu as pltpu
from jax.sharding import PartitionSpec as P

KEEP_SCALE = 4.0 / 3.0
SWAP = [(0, 1), (1, 0)]
TN = (((0,), (0,)), ((), ()))
NT = (((1,), (1,)), ((), ()))
CHUNKS = 4
PARAMS = pltpu.CompilerParams(vmem_limit_bytes=16 * 2**20)
VMEM = pl.BlockSpec(memory_space=pltpu.VMEM)
ANY = pl.BlockSpec(memory_space=pl.ANY)
SMEM = pl.BlockSpec(memory_space=pltpu.SMEM)


def resident(array):
    return pltpu.with_memory_space_constraint(array, pltpu.VMEM)


def in_hbm(array):
    return pltpu.with_memory_space_constraint(array, pltpu.HBM)


def cut(ref, dim, index, count):
    size = ref.shape[dim] // count
    part = pl.ds(index * size, size)
    return ref.at[part, :] if dim == 0 else ref.at[:, part]


def half_of(ref, which):
    half = ref.shape[1] // 2
    return ref.at[:, pl.ds(pl.multiple_of(which * half, half), half)]


def part_of_product(dim, c, rows, columns):
    left, right = (cut(rows, 1, c, CHUNKS), columns) if dim == 0 else (rows, cut(columns, 1, c, CHUNKS))
    return lax.dot_general(left[...], right[...], TN, preferred_element_type=jnp.float32)


def far_kernel(dim, which_ref, rows, columns, *outs):
    half = rows.shape[1] // 2
    for c in range(CHUNKS):
        total = part_of_product(dim, c, half_of(rows, which_ref[0]), columns)
        cut(outs[c // 2], dim, c % 2, 2)[...] = total.astype(jnp.bfloat16)


def near_kernel(dim, which_ref, rows, columns, first, second, out_hbm, out, sem, *held):
    rows = half_of(rows, which_ref[0])
    if dim == 1:
        arrival = pltpu.make_async_copy(rows, held[0], held[1])
        arrival.start()
        rows = held[0]
        arrival.wait()
    departures = []
    for c in range(CHUNKS):
        far = cut((first, second)[c // 2], dim, c % 2, 2)
        total = part_of_product(dim, c, rows, columns)
        cut(out, dim, c, CHUNKS)[...] = total + far[...].astype(jnp.float32)
        departure = pltpu.make_async_copy(
            cut(out, dim, c, CHUNKS), cut(out_hbm, dim, c, CHUNKS), sem.at[c]
        )
        departure.start()
        departures.append(departure)
    for departure in departures:
        departure.wait()


def half_product(which, rows, columns, dim, far=None):
    half, wide = rows.shape[1] // 2, columns.shape[1]
    if far is None:
        piece = (half // 2, wide) if dim == 0 else (half, wide // 2)
        return pl.pallas_call(
            functools.partial(far_kernel, dim),
            out_shape=[pltpu.VMEM(piece, jnp.bfloat16)] * 2,
            in_specs=[SMEM, VMEM, VMEM],
            out_specs=[VMEM] * 2,
            compiler_params=PARAMS,
            name="far_product",
        )(which, resident(rows), resident(columns))
    return pl.pallas_call(
        functools.partial(near_kernel, dim),
        out_shape=jax.ShapeDtypeStruct((half, wide), jnp.float32),
        in_specs=[SMEM, VMEM if dim == 0 else ANY] + [VMEM] * 3,
        out_specs=ANY,
        scratch_shapes=[
            pltpu.VMEM((half, wide), jnp.float32),
            pltpu.SemaphoreType.DMA((CHUNKS,)),
            *([] if dim == 0 else [pltpu.VMEM((rows.shape[0], half), jnp.bfloat16), pltpu.SemaphoreType.DMA]),
        ],
        compiler_params=PARAMS,
        name="near_product",
    )(which, resident(rows) if dim == 0 else in_hbm(rows), resident(columns), resident(far[0]), resident(far[1]))


def backward_kernel(which_ref, grads, weight, slope, rows_hbm, dpre, first, second, rows, sem):
    far = (first, second)
    arrival = pltpu.make_async_copy(half_of(rows_hbm, which_ref[0]), rows, sem)
    arrival.start()
    for c in range(CHUNKS):
        for r in range(4):
            dhidden = lax.dot_general(
                cut(grads, 0, r, 4)[...], cut(weight, 0, c, CHUNKS)[...], NT, preferred_element_type=jnp.float32
            )
            factor = cut(cut(slope, 1, c, CHUNKS), 0, r, 4)[...].astype(jnp.float32)
            cut(cut(dpre, 1, c, CHUNKS), 0, r, 4)[...] = (dhidden * factor).astype(jnp.bfloat16)
        if c == 0:
            arrival.wait()
        share = part_of_product(1, c, rows, dpre)
        cut(far[c // 2], 1, c % 2, 2)[...] = share.astype(jnp.bfloat16)


def backward(which, grads, weight, slope, rows):
    depth, width = grads.shape
    hidden, half = slope.shape[1], width // 2
    piece = pltpu.VMEM((half, hidden // 2), jnp.bfloat16)
    return pl.pallas_call(
        backward_kernel,
        out_shape=[pltpu.VMEM((depth, hidden), jnp.bfloat16), piece, piece],
        in_specs=[SMEM] + [VMEM] * 3 + [ANY],
        out_specs=[VMEM] * 3,
        scratch_shapes=[pltpu.VMEM((depth, half), jnp.bfloat16), pltpu.SemaphoreType.DMA],
        compiler_params=PARAMS,
        name="backward",
    )(which, *map(resident, (grads, weight, slope)), in_hbm(rows))


def route_kernel(
    experts, capacity, ids_hbm, tokens_hbm, target_ref, sent_hbm, named, tokens, sent, in_sem, out_sem
):
    naming = pltpu.make_async_copy(ids_hbm, named, in_sem.at[0])
    naming.start()
    arrival = pltpu.make_async_copy(tokens_hbm, tokens, in_sem.at[1])
    arrival.start()
    naming.wait()
    ids = named[...]
    count = ids.shape[1]
    chosen = lax.broadcasted_iota(jnp.int32, (experts, count), 0) == ids
    chosen = jnp.where(chosen, 1.0, 0.0)
    earlier = lax.broadcasted_iota(jnp.int32, (count, count), 0) < lax.broadcasted_iota(
        jnp.int32, (count, count), 1
    )
    earlier = jnp.where(earlier, 1.0, 0.0).astype(jnp.bfloat16)
    ahead = jnp.dot(chosen.astype(jnp.bfloat16), earlier, preferred_element_type=jnp.float32)
    rank = jnp.sum(chosen * ahead, axis=0, keepdims=True)
    target = ids * capacity + rank.astype(jnp.int32)
    target_ref[...] = target
    arrival.wait()
    size = sent.shape[0] // CHUNKS
    departures = []
    for c in range(CHUNKS):
        row = lax.broadcasted_iota(jnp.int32, (size, count), 0) + c * size
        select = jnp.where(row == target, 1.0, 0.0).astype(jnp.bfloat16)
        filled = jnp.dot(select, tokens[...], preferred_element_type=jnp.float32)
        cut(sent, 0, c, CHUNKS)[...] = filled.astype(jnp.bfloat16)
        departure = pltpu.make_async_copy(
            cut(sent, 0, c, CHUNKS), cut(sent_hbm, 0, c, CHUNKS), out_sem.at[c]
        )
        departure.start()
        departures.append(departure)
    for departure in departures:
        departure.wait()


def route(ids, tokens, experts, capacity):
    filled = (experts * capacity, tokens.shape[1])
    return pl.pallas_call(
        functools.partial(route_kernel, experts, capacity),
        out_shape=[
            jax.ShapeDtypeStruct(ids.shape, jnp.int32),
            pltpu.HBM(filled, jnp.bfloat16),
        ],
        in_specs=[ANY, ANY],
        out_specs=[VMEM, ANY],
        scratch_shapes=[
            pltpu.VMEM(ids.shape, jnp.int32),
            pltpu.VMEM(tokens.shape, jnp.bfloat16),
            pltpu.VMEM(filled, jnp.bfloat16),
            pltpu.SemaphoreType.DMA((2,)),
            pltpu.SemaphoreType.DMA((CHUNKS,)),
        ],
        compiler_params=PARAMS,
        name="route",
    )(in_hbm(ids), in_hbm(tokens))


def mix_kernel(target_ref, prob_ref, back_ref, mixed_hbm, mixed, sem):
    slots, count = back_ref.shape[0], mixed.shape[0] // 2
    departures = []
    for c in range(2):
        tokens = pl.ds(c * count, count)
        slot = lax.broadcasted_iota(jnp.int32, (count, slots), 1)
        select = jnp.where(slot == target_ref[tokens, :1], 1.0, 0.0).astype(jnp.bfloat16)
        out = jnp.dot(select, back_ref[...], preferred_element_type=jnp.float32)
        mixed[tokens, :] = (prob_ref[tokens, :1] * out).astype(jnp.bfloat16)
        departure = pltpu.make_async_copy(mixed.at[tokens, :], mixed_hbm.at[tokens, :], sem.at[c])
        departure.start()
        departures.append(departure)
    for departure in departures:
        departure.wait()


def mix(target, prob, back):
    shape = (target.shape[0], back.shape[1])
    return pl.pallas_call(
        mix_kernel,
        out_shape=jax.ShapeDtypeStruct(shape, jnp.bfloat16),
        in_specs=[VMEM] * 3,
        out_specs=ANY,
        scratch_shapes=[pltpu.VMEM(shape, jnp.bfloat16), pltpu.SemaphoreType.DMA((2,))],
        compiler_params=PARAMS,
        name="mix",
    )(resident(target), resident(prob), resident(back))


def gelu_parts(pre):
    inner = 0.7978845608 * (pre + 0.044715 * pre * pre * pre)
    tanh_v = jnp.tanh(inner)
    value = 0.5 * pre * (1.0 + tanh_v)
    slope = 0.5 * (1.0 + tanh_v) + 0.5 * pre * (1.0 - tanh_v * tanh_v) * 0.7978845608 * (
        1.0 + 3.0 * 0.044715 * pre * pre
    )
    return (value, slope)


def exchange(array):
    return lax.all_to_all(array, "expert", split_axis=0, concat_axis=0, tiled=True)


def swapped(pieces):
    return [lax.ppermute(piece, "replica", SWAP) for piece in pieces]


def shards(tokens, expert_id, router_prob, keep_mask, w_in, w_out, cotangent):
    tok_rows, width = tokens.shape
    n_expert = lax.axis_size("expert")
    n_replica = lax.axis_size("replica")
    capacity = 2 * tok_rows // n_expert
    slots = n_expert * capacity
    weight_in = w_in[0]
    weight_out = w_out[0]
    ids = expert_id.reshape(1, tok_rows)
    target, sent = route(ids, tokens, n_expert, capacity)
    sent = sent.reshape(n_expert, capacity, width)
    gated = (router_prob[:, None] * cotangent.astype(jnp.float32)).astype(jnp.bfloat16)
    keep_rows = lax.dynamic_index_in_dim(
        keep_mask[0].reshape(n_expert, n_replica, -1),
        lax.axis_index("replica"),
        axis=1,
        keepdims=False,
    )
    keep_scale = keep_rows.astype(jnp.float32) * KEEP_SCALE
    select = jnp.arange(slots, dtype=jnp.int32)[:, None] == target
    sent_grad = jnp.dot(select.astype(jnp.bfloat16), gated, preferred_element_type=jnp.float32)
    sent_grad = sent_grad.astype(jnp.bfloat16).reshape(n_expert, capacity, width)
    prob = jnp.broadcast_to(router_prob[:, None], (tok_rows, 128))
    column = jnp.broadcast_to(target.reshape(tok_rows, 1), (tok_rows, 128))
    received = exchange(sent).reshape(slots, width)
    sent_grad, keep_scale, prob, column = lax.optimization_barrier(
        (sent_grad, keep_scale, prob, column)
    )
    grad_rows = exchange(sent_grad).reshape(slots, width)
    keep_scale = jnp.broadcast_to(keep_scale[:, None, :], (n_expert, capacity, keep_scale.shape[1]))
    keep_scale = keep_scale.reshape(slots, -1)
    pre = jnp.dot(received, weight_in, preferred_element_type=jnp.float32)
    value, slope = gelu_parts(pre)
    hidden = (value * keep_scale).astype(jnp.bfloat16)
    slope = (slope * keep_scale).astype(jnp.bfloat16)
    out = jnp.dot(hidden, weight_out, preferred_element_type=jnp.float32).astype(jnp.bfloat16)
    out, grad_rows = lax.optimization_barrier((out, grad_rows))
    back = exchange(out.reshape(n_expert, capacity, width)).reshape(slots, width)
    here = lax.axis_index("replica").reshape(1)
    other = 1 - here
    dpre, *far_in = backward(other, grad_rows, weight_out, slope, received)
    far_in = swapped(far_in)
    far_out = swapped(half_product(other, hidden, grad_rows, 0))
    grad_in = half_product(here, received, dpre, 1, far_in)
    grad_out = half_product(here, hidden, grad_rows, 0, far_out)
    back, grad_in, grad_out = lax.optimization_barrier((back, grad_in, grad_out))
    mixed = mix(column, prob, back)
    return (mixed, grad_in[None], grad_out[None])


def solution(mesh):
    in_specs = (
        P(("expert", "replica"), None),
        P(("expert", "replica"), None),
        P(("expert", "replica")),
        P("expert", None, None),
        P("expert", None, None),
        P("expert", None, None),
        P(("expert", "replica"), None),
    )
    out_specs = (
        P(("expert", "replica"), None),
        P("expert", "replica", None),
        P("expert", "replica", None),
    )
    return jax.shard_map(shards, mesh=mesh, in_specs=in_specs, out_specs=out_specs, check_vma=False)
```

```python
import functools

import jax
import jax.numpy as jnp
from jax import lax
from jax.experimental import pallas as pl
from jax.experimental.pallas import tpu as pltpu
from jax.sharding import PartitionSpec as P

KEEP_SCALE = 4.0 / 3.0
SWAP = [(0, 1), (1, 0)]
TN = (((0,), (0,)), ((), ()))
NT = (((1,), (1,)), ((), ()))
CHUNKS = 4
PARAMS = pltpu.CompilerParams(vmem_limit_bytes=16 * 2**20)
VMEM = pl.BlockSpec(memory_space=pltpu.VMEM)
ANY = pl.BlockSpec(memory_space=pl.ANY)
SMEM = pl.BlockSpec(memory_space=pltpu.SMEM)


def resident(array):
    return pltpu.with_memory_space_constraint(array, pltpu.VMEM)


def in_hbm(array):
    return pltpu.with_memory_space_constraint(array, pltpu.HBM)


def cut(ref, dim, index, count):
    size = ref.shape[dim] // count
    part = pl.ds(index * size, size)
    return ref.at[part, :] if dim == 0 else ref.at[:, part]


def half_of(ref, which):
    half = ref.shape[1] // 2
    return ref.at[:, pl.ds(pl.multiple_of(which * half, half), half)]


def part_of_product(dim, c, rows, columns):
    left, right = (cut(rows, 1, c, CHUNKS), columns) if dim == 0 else (rows, cut(columns, 1, c, CHUNKS))
    return lax.dot_general(left[...], right[...], TN, preferred_element_type=jnp.float32)


def far_kernel(dim, which_ref, rows, columns, *outs):
    half = rows.shape[1] // 2
    for c in range(CHUNKS):
        total = part_of_product(dim, c, half_of(rows, which_ref[0]), columns)
        cut(outs[c // 2], dim, c % 2, 2)[...] = total.astype(jnp.bfloat16)


def near_kernel(dim, which_ref, rows, columns, first, second, out_hbm, out, sem, *held):
    rows = half_of(rows, which_ref[0])
    if dim == 1:
        arrival = pltpu.make_async_copy(rows, held[0], held[1])
        arrival.start()
        rows = held[0]
        arrival.wait()
    departures = []
    for c in range(CHUNKS):
        far = cut((first, second)[c // 2], dim, c % 2, 2)
        total = part_of_product(dim, c, rows, columns)
        cut(out, dim, c, CHUNKS)[...] = total + far[...].astype(jnp.float32)
        departure = pltpu.make_async_copy(
            cut(out, dim, c, CHUNKS), cut(out_hbm, dim, c, CHUNKS), sem.at[c]
        )
        departure.start()
        departures.append(departure)
    for departure in departures:
        departure.wait()


def half_product(which, rows, columns, dim, far=None):
    half, wide = rows.shape[1] // 2, columns.shape[1]
    if far is None:
        piece = (half // 2, wide) if dim == 0 else (half, wide // 2)
        return pl.pallas_call(
            functools.partial(far_kernel, dim),
            out_shape=[pltpu.VMEM(piece, jnp.bfloat16)] * 2,
            in_specs=[SMEM, VMEM, VMEM],
            out_specs=[VMEM] * 2,
            compiler_params=PARAMS,
            name="far_product",
        )(which, resident(rows), resident(columns))
    return pl.pallas_call(
        functools.partial(near_kernel, dim),
        out_shape=jax.ShapeDtypeStruct((half, wide), jnp.float32),
        in_specs=[SMEM, VMEM if dim == 0 else ANY] + [VMEM] * 3,
        out_specs=ANY,
        scratch_shapes=[
            pltpu.VMEM((half, wide), jnp.float32),
            pltpu.SemaphoreType.DMA((CHUNKS,)),
            *([] if dim == 0 else [pltpu.VMEM((rows.shape[0], half), jnp.bfloat16), pltpu.SemaphoreType.DMA]),
        ],
        compiler_params=PARAMS,
        name="near_product",
    )(which, resident(rows) if dim == 0 else in_hbm(rows), resident(columns), resident(far[0]), resident(far[1]))


def backward_kernel(which_ref, grads, weight, slope, rows_hbm, dpre, first, second, rows, sem):
    far = (first, second)
    arrival = pltpu.make_async_copy(half_of(rows_hbm, which_ref[0]), rows, sem)
    arrival.start()
    for c in range(CHUNKS):
        for r in range(4):
            dhidden = lax.dot_general(
                cut(grads, 0, r, 4)[...], cut(weight, 0, c, CHUNKS)[...], NT, preferred_element_type=jnp.float32
            )
            factor = cut(cut(slope, 1, c, CHUNKS), 0, r, 4)[...].astype(jnp.float32)
            cut(cut(dpre, 1, c, CHUNKS), 0, r, 4)[...] = (dhidden * factor).astype(jnp.bfloat16)
        if c == 0:
            arrival.wait()
        share = part_of_product(1, c, rows, dpre)
        cut(far[c // 2], 1, c % 2, 2)[...] = share.astype(jnp.bfloat16)


def backward(which, grads, weight, slope, rows):
    depth, width = grads.shape
    hidden, half = slope.shape[1], width // 2
    piece = pltpu.VMEM((half, hidden // 2), jnp.bfloat16)
    return pl.pallas_call(
        backward_kernel,
        out_shape=[pltpu.VMEM((depth, hidden), jnp.bfloat16), piece, piece],
        in_specs=[SMEM] + [VMEM] * 3 + [ANY],
        out_specs=[VMEM] * 3,
        scratch_shapes=[pltpu.VMEM((depth, half), jnp.bfloat16), pltpu.SemaphoreType.DMA],
        compiler_params=PARAMS,
        name="backward",
    )(which, *map(resident, (grads, weight, slope)), in_hbm(rows))


def route_kernel(
    experts, capacity, ids_hbm, tokens_hbm, target_ref, sent_hbm, named, tokens, sent, in_sem, out_sem
):
    naming = pltpu.make_async_copy(ids_hbm, named, in_sem.at[0])
    naming.start()
    arrival = pltpu.make_async_copy(tokens_hbm, tokens, in_sem.at[1])
    arrival.start()
    naming.wait()
    ids = named[...]
    count = ids.shape[1]
    chosen = lax.broadcasted_iota(jnp.int32, (experts, count), 0) == ids
    chosen = jnp.where(chosen, 1.0, 0.0)
    earlier = lax.broadcasted_iota(jnp.int32, (count, count), 0) < lax.broadcasted_iota(
        jnp.int32, (count, count), 1
    )
    earlier = jnp.where(earlier, 1.0, 0.0).astype(jnp.bfloat16)
    ahead = jnp.dot(chosen.astype(jnp.bfloat16), earlier, preferred_element_type=jnp.float32)
    rank = jnp.sum(chosen * ahead, axis=0, keepdims=True)
    target = ids * capacity + rank.astype(jnp.int32)
    target_ref[...] = target
    arrival.wait()
    size = sent.shape[0] // CHUNKS
    departures = []
    for c in range(CHUNKS):
        row = lax.broadcasted_iota(jnp.int32, (size, count), 0) + c * size
        select = jnp.where(row == target, 1.0, 0.0).astype(jnp.bfloat16)
        filled = jnp.dot(select, tokens[...], preferred_element_type=jnp.float32)
        cut(sent, 0, c, CHUNKS)[...] = filled.astype(jnp.bfloat16)
        departure = pltpu.make_async_copy(
            cut(sent, 0, c, CHUNKS), cut(sent_hbm, 0, c, CHUNKS), out_sem.at[c]
        )
        departure.start()
        departures.append(departure)
    for departure in departures:
        departure.wait()


def route(ids, tokens, experts, capacity):
    filled = (experts * capacity, tokens.shape[1])
    return pl.pallas_call(
        functools.partial(route_kernel, experts, capacity),
        out_shape=[
            jax.ShapeDtypeStruct(ids.shape, jnp.int32),
            pltpu.HBM(filled, jnp.bfloat16),
        ],
        in_specs=[ANY, ANY],
        out_specs=[VMEM, ANY],
        scratch_shapes=[
            pltpu.VMEM(ids.shape, jnp.int32),
            pltpu.VMEM(tokens.shape, jnp.bfloat16),
            pltpu.VMEM(filled, jnp.bfloat16),
            pltpu.SemaphoreType.DMA((2,)),
            pltpu.SemaphoreType.DMA((CHUNKS,)),
        ],
        compiler_params=PARAMS,
        name="route",
    )(in_hbm(ids), in_hbm(tokens))


def mix_kernel(target_ref, prob_ref, back_hbm, mixed_ref, back, in_sem):
    parts = 2
    count = back.shape[0] // parts
    arrivals = [
        pltpu.make_async_copy(cut(back_hbm, 0, c, parts), cut(back, 0, c, parts), in_sem.at[c])
        for c in range(parts)
    ]
    for arrival in arrivals:
        arrival.start()
    total = None
    for c in range(parts):
        slot = lax.broadcasted_iota(jnp.int32, (mixed_ref.shape[0], count), 1) + c * count
        select = jnp.where(slot == target_ref[:, :1], 1.0, 0.0).astype(jnp.bfloat16)
        arrivals[c].wait()
        out = jnp.dot(select, cut(back, 0, c, parts)[...], preferred_element_type=jnp.float32)
        total = out if total is None else total + out
    mixed_ref[...] = (prob_ref[:, :1] * total).astype(jnp.bfloat16)


def mix(target, prob, back):
    return pl.pallas_call(
        mix_kernel,
        out_shape=jax.ShapeDtypeStruct((target.shape[0], back.shape[1]), jnp.bfloat16),
        in_specs=[VMEM, VMEM, ANY],
        out_specs=VMEM,
        scratch_shapes=[pltpu.VMEM(back.shape, jnp.bfloat16), pltpu.SemaphoreType.DMA((2,))],
        compiler_params=PARAMS,
        name="mix",
    )(resident(target), resident(prob), in_hbm(back))


def gelu_parts(pre):
    inner = 0.7978845608 * (pre + 0.044715 * pre * pre * pre)
    tanh_v = jnp.tanh(inner)
    value = 0.5 * pre * (1.0 + tanh_v)
    slope = 0.5 * (1.0 + tanh_v) + 0.5 * pre * (1.0 - tanh_v * tanh_v) * 0.7978845608 * (
        1.0 + 3.0 * 0.044715 * pre * pre
    )
    return (value, slope)


def exchange(array):
    return lax.all_to_all(array, "expert", split_axis=0, concat_axis=0, tiled=True)


def swapped(pieces):
    return [lax.ppermute(piece, "replica", SWAP) for piece in pieces]


def shards(tokens, expert_id, router_prob, keep_mask, w_in, w_out, cotangent):
    tok_rows, width = tokens.shape
    n_expert = lax.axis_size("expert")
    n_replica = lax.axis_size("replica")
    capacity = 2 * tok_rows // n_expert
    slots = n_expert * capacity
    weight_in = w_in[0]
    weight_out = w_out[0]
    ids = expert_id.reshape(1, tok_rows)
    target, sent = route(ids, tokens, n_expert, capacity)
    sent = sent.reshape(n_expert, capacity, width)
    gated = (router_prob[:, None] * cotangent.astype(jnp.float32)).astype(jnp.bfloat16)
    keep_rows = lax.dynamic_index_in_dim(
        keep_mask[0].reshape(n_expert, n_replica, -1),
        lax.axis_index("replica"),
        axis=1,
        keepdims=False,
    )
    keep_scale = keep_rows.astype(jnp.float32) * KEEP_SCALE
    select = jnp.arange(slots, dtype=jnp.int32)[:, None] == target
    sent_grad = jnp.dot(select.astype(jnp.bfloat16), gated, preferred_element_type=jnp.float32)
    sent_grad = sent_grad.astype(jnp.bfloat16).reshape(n_expert, capacity, width)
    prob = jnp.broadcast_to(router_prob[:, None], (tok_rows, 128))
    column = jnp.broadcast_to(target.reshape(tok_rows, 1), (tok_rows, 128))
    received = exchange(sent).reshape(slots, width)
    sent_grad, keep_scale, prob, column = lax.optimization_barrier(
        (sent_grad, keep_scale, prob, column)
    )
    grad_rows = exchange(sent_grad).reshape(slots, width)
    keep_scale = jnp.broadcast_to(keep_scale[:, None, :], (n_expert, capacity, keep_scale.shape[1]))
    keep_scale = keep_scale.reshape(slots, -1)
    pre = jnp.dot(received, weight_in, preferred_element_type=jnp.float32)
    value, slope = gelu_parts(pre)
    hidden = (value * keep_scale).astype(jnp.bfloat16)
    slope = (slope * keep_scale).astype(jnp.bfloat16)
    out = jnp.dot(hidden, weight_out, preferred_element_type=jnp.float32).astype(jnp.bfloat16)
    out, grad_rows = lax.optimization_barrier((out, grad_rows))
    back = exchange(out.reshape(n_expert, capacity, width)).reshape(slots, width)
    here = lax.axis_index("replica").reshape(1)
    other = 1 - here
    dpre, *far_in = backward(other, grad_rows, weight_out, slope, received)
    far_in = swapped(far_in)
    far_out = swapped(half_product(other, hidden, grad_rows, 0))
    grad_in = half_product(here, received, dpre, 1, far_in)
    grad_out = half_product(here, hidden, grad_rows, 0, far_out)
    back, grad_in, grad_out = lax.optimization_barrier((back, grad_in, grad_out))
    mixed = mix(column, prob, back)
    return (mixed, grad_in[None], grad_out[None])


def solution(mesh):
    in_specs = (
        P(("expert", "replica"), None),
        P(("expert", "replica"), None),
        P(("expert", "replica")),
        P("expert", None, None),
        P("expert", None, None),
        P("expert", None, None),
        P(("expert", "replica"), None),
    )
    out_specs = (
        P(("expert", "replica"), None),
        P("expert", "replica", None),
        P("expert", "replica", None),
    )
    return jax.shard_map(shards, mesh=mesh, in_specs=in_specs, out_specs=out_specs, check_vma=False)
```
